32 devices in a mesh: span: 4 (over y, x), tensor: 8 (over z, core).
Axes of the slice: x: 2, y: 2, z: 4, core: 2. Of those that a mesh axis runs over, the one named last changes fastest.
Arguments:
- tokens: bfloat16 [1024, 4096], P('span', 'tensor'), may hold values from -200 to 200
- retain: float32 [1024], P('span'), may hold values from 0.5 to 1
- norm_gain: float32 [4096], P('tensor'), may hold values from 0.1 to 1.9
- norm_bias: float32 [4096], P('tensor'), may hold values from -2.5 to 2.5
- decay_rate: float32 [16, 4096], P(None, 'tensor'), may hold values from 0.00024414062 to 0.0333333333
- ema_angle: float32 [16, 4096], P(None, 'tensor'), may hold values from -0.05 to 0.05
- ema_input: float32 [16, 4096], P(None, 'tensor'), may hold values from -2.4 to 2.4
- ema_output: float32 [2, 16, 4096], P(None, None, 'tensor'), may hold values from -0.25 to 0.25
- ema_skip: float32 [4096], P('tensor'), may hold values from -3 to 3
- shared_weight: bfloat16 [4096, 1024], P('tensor'), may hold values from -0.125 to 0.125
- shared_gain: float32 [1024], replicated, may hold values from 0.1 to 1.9
- output_weight: bfloat16 [1024, 4096], P(None, 'tensor'), may hold values from -0.1875 to 0.1875
Outputs:
- layer_out: bfloat16 [1024, 4096], P('span', 'tensor')
The draws below stay inside these ranges and needn't reach their ends.
All inputs are finite; a program needn't handle non-finite values.
Results may differ from the reference program's by a relative error of at most 0.02.
Values may be sent and summed in bfloat16 or wider, within the bound.
A program may use at most 128 MiB of HBM per device.

```python
import jax
import jax.numpy as jnp
from jax import lax

D = 4096
NDIM = 16
Z = 1024
GROUP = 64
BLOCK = 64
STREAM_LENGTH = 1024
N_TENSOR = 8


def draw_tokens(key, part):
    random_seed_list = jax.random.split(jax.random.fold_in(key, 11), 3)
    element_ordinal = jnp.arange(STREAM_LENGTH).astype(jnp.float32) / STREAM_LENGTH
    column_scale = jnp.exp(jax.random.uniform(random_seed_list[0], (D,), minval=0.0, maxval=jnp.log(10.0)))
    start_offset = jnp.clip(jax.random.normal(random_seed_list[1], (D,)), -3.0, 3.0) * 0.7
    growth = 1.0 + 2.0 * element_ordinal
    jitter = jnp.clip(jax.random.normal(random_seed_list[2], (STREAM_LENGTH, D)), -6.0, 6.0)
    values = growth[:, None] * column_scale[None] * (start_offset[None] + jitter)
    return jnp.clip(values, -200.0, 200.0).astype(jnp.bfloat16)


def draw_retain(key, part):
    random_seed_list = jax.random.split(jax.random.fold_in(key, 23), 2)
    peak_spot_index = jax.random.permutation(random_seed_list[0], STREAM_LENGTH)[:8]
    levels = jax.random.uniform(random_seed_list[1], (8,), minval=0.5, maxval=0.7)
    levels = levels.at[0].set(0.5)
    element_ordinal = jnp.arange(STREAM_LENGTH)
    agreeing_outcome = element_ordinal[:, None] == peak_spot_index[None]
    factor = jnp.min(jnp.where(agreeing_outcome, levels[None], 1.0), axis=1)
    return factor.astype(jnp.float32)


def ema_rates(key):
    random_seed_list = jax.random.split(jax.random.fold_in(key, 37), 3)
    chooser = jax.random.uniform(random_seed_list[0], (NDIM, D))
    fast_rate = jnp.exp(jax.random.uniform(random_seed_list[1], (NDIM, D), minval=jnp.log(1.0 / 50), maxval=jnp.log(1.0 / 30)))
    fast_share = 0.25
    slow_top = 4.0
    slow_rate = jnp.exp(jax.random.uniform(random_seed_list[2], (NDIM, D), minval=jnp.log(0.25 / STREAM_LENGTH), maxval=jnp.log(slow_top / STREAM_LENGTH)))
    return jnp.where(chooser < fast_share, fast_rate, slow_rate)


def channel_sign(key):
    flips = jax.random.randint(jax.random.fold_in(key, 53), (D,), 0, 2)
    return (2 * flips - 1).astype(jnp.float32)


def draw_decay_rate(key, part):
    return ema_rates(key).astype(jnp.float32)


def draw_ema_angle(key, part):
    reach = 1.0
    turn = jax.random.uniform(jax.random.fold_in(key, 41), (NDIM, D), minval=-reach, maxval=reach)
    return (ema_rates(key) * turn).astype(jnp.float32)


def draw_ema_input(key, part):
    low, high = (1.0, 2.0)
    size_part = jax.random.uniform(jax.random.fold_in(key, 61), (NDIM, D), minval=low, maxval=high)
    return (channel_sign(key)[None] * size_part).astype(jnp.float32)


def draw_ema_output(key, part):
    random_seed_list = jax.random.split(jax.random.fold_in(key, 67), 2)
    low, high = (0.1, 0.2)
    real_part = channel_sign(key)[None] * jax.random.uniform(random_seed_list[0], (NDIM, D), minval=low, maxval=high)
    imag_part = jax.random.uniform(random_seed_list[1], (NDIM, D), minval=-0.1, maxval=0.1)
    return jnp.stack([real_part, imag_part]).astype(jnp.float32)


def draw_norm_bias(key, part):
    random_seed_list = jax.random.split(jax.random.fold_in(key, 71), 2)
    low, high = (1.0, 2.0)
    flips = jax.random.randint(random_seed_list[0], (D,), 0, 2)
    size_part = jax.random.uniform(random_seed_list[1], (D,), minval=low, maxval=high)
    return ((2 * flips - 1).astype(jnp.float32) * size_part).astype(jnp.float32)


def strengthened(values, key, source, target, shards_of, factor):
    def block_of(axis_at):
        return (jnp.arange(values.shape[axis_at]) // (values.shape[axis_at] // shards_of)).reshape((-1,) + (1,) * (values.ndim - 1 - axis_at))

    one_side = jax.random.permutation(key, shards_of)[block_of(target)]
    other_side = (block_of(target) + shards_of // 2) % shards_of
    return jnp.where((block_of(source) == one_side) | (block_of(source) == other_side), factor * values, values)


def level_of(key, shape, cuts, smallest, largest):
    def one(position, parts):
        draws = jax.random.uniform(jax.random.fold_in(jax.random.fold_in(key, 6), position), (parts,), jnp.float32, smallest / len(cuts), largest / len(cuts))
        return jnp.repeat(jnp.exp(draws), shape[position] // parts).reshape((-1,) + (1,) * (len(shape) - position - 1))

    loudness = one(*cuts[0])
    for cut in cuts[1:]:
        loudness = loudness * one(*cut)
    return loudness


def scatter_about(stream_key, extent, scale, most, pieces=(), kind=jnp.bfloat16):
    array = jax.random.normal(stream_key, extent, jnp.float32) * scale
    if len(pieces) > 0:
        array = level_of(stream_key, extent, pieces, -0.22, 0.18) * array
    return jnp.clip(array, min=-most, max=most).astype(kind)


def heavy_noise(own_key, extent, scale, bound, cuts, heavy, held_as=jnp.bfloat16):
    entries = scale * jax.random.normal(own_key, extent, jnp.float32)
    if cuts:
        entries = entries * level_of(own_key, extent, cuts, -0.22, 0.18)
    return jnp.clip(strengthened(entries, jax.random.fold_in(own_key, 3), *heavy), -bound, bound).astype(held_as)


def setup_inputs(seed: int = 0) -> dict:
    streams_of = jax.random.split(jax.random.key(seed), 13)
    return {
        "tokens": draw_tokens(jax.random.fold_in(streams_of[12], 71), 0),
        "retain": draw_retain(jax.random.fold_in(streams_of[12], 71), 0),
        "norm_gain": jnp.clip(1.0 + 0.18 * jax.random.normal(streams_of[2], (D,), jnp.float32), 0.1, 1.9),
        "norm_bias": draw_norm_bias(jax.random.fold_in(streams_of[12], 71), 0),
        "decay_rate": draw_decay_rate(jax.random.fold_in(streams_of[12], 71), 0),
        "ema_angle": draw_ema_angle(jax.random.fold_in(streams_of[12], 71), 0),
        "ema_input": draw_ema_input(jax.random.fold_in(streams_of[12], 71), 0),
        "ema_output": draw_ema_output(jax.random.fold_in(streams_of[12], 71), 0),
        "ema_skip": scatter_about(streams_of[8], (D,), 0.5, 3.0, ((0, 8),), jnp.float32),
        "shared_weight": heavy_noise(streams_of[9], (D, Z), D ** -0.5, 0.125, ((0, 8),), (0, 1, 8, 2.0)),
        "shared_gain": jnp.clip(1.0 + 0.18 * jax.random.normal(streams_of[10], (Z,), jnp.float32), 0.1, 1.9),
        "output_weight": scatter_about(streams_of[11], (Z, D), Z ** -0.5, 0.1875, ((1, 8),)),
    }


precise = lax.Precision.HIGHEST
norm_eps = 1e-05
scale_eps = 1e-06

def lag_powers(decay_rate, ema_angle, count):
    lag_steps = jnp.arange(count, dtype=jnp.int32).astype(jnp.float32)[:, None, None]
    magnitude = jnp.exp(-decay_rate[None] * lag_steps)
    return (magnitude * jnp.cos(ema_angle[None] * lag_steps), magnitude * jnp.sin(ema_angle[None] * lag_steps))

def toeplitz(kernel):
    width = kernel.shape[0]
    flipped = jnp.concatenate([kernel[::-1], jnp.zeros_like(kernel)], axis=0)
    repeated = jnp.tile(flipped, (width, 1))[:width * (2 * width - 1)]
    return repeated.reshape(width, 2 * width - 1, kernel.shape[1])[:, width - 1:2 * width - 1]

def block_combine(earlier, later):
    mult_re = later[0] * earlier[0] - later[1] * earlier[1]
    mult_im = later[0] * earlier[1] + later[1] * earlier[0]
    add_re = later[0] * earlier[2] - later[1] * earlier[3] + later[2]
    add_im = later[0] * earlier[3] + later[1] * earlier[2] + later[3]
    return (mult_re, mult_im, add_re, add_im)

def group_terms(tokens):
    values = tokens.astype(jnp.float32)
    grouped = values.reshape(values.shape[0], -1, GROUP)
    return (grouped, lax.optimization_barrier(jnp.sum(grouped, axis=2)), lax.optimization_barrier(jnp.sum(grouped * grouped, axis=2)))

def timestep_norm(grouped, group_sums, group_squares, before, first_row, norm_gain, norm_bias):
    length = grouped.shape[0]
    cum_sum = before[0][None] + jnp.cumsum(group_sums, axis=0)
    cum_sq = before[1][None] + jnp.cumsum(group_squares, axis=0)
    counts = ((first_row + jnp.arange(length, dtype=jnp.int32) + 1) * GROUP).astype(jnp.float32)[:, None]
    average = cum_sum / counts
    spread = cum_sq / counts - average * average
    inverse = lax.rsqrt(spread + norm_eps)
    normed = (grouped - average[:, :, None]) * inverse[:, :, None]
    return normed.reshape(length, -1) * norm_gain[None] + norm_bias[None]

def ema_local(normed, retain, decay_rate, ema_angle, ema_input, ema_output):
    length, channels = normed.shape
    blocks = length // BLOCK
    power_real, power_im = lag_powers(decay_rate, ema_angle, BLOCK + 1)
    weight = (1.0 - jnp.exp(-decay_rate)) * ema_input
    kernel = lax.optimization_barrier(jnp.sum(weight[None] * (ema_output[0][None] * power_real[:BLOCK] - ema_output[1][None] * power_im[:BLOCK]), axis=1))
    matrix = toeplitz(kernel)
    retained = jnp.cumprod(retain.reshape(blocks, BLOCK), axis=1)
    scaled = normed.reshape(blocks, BLOCK, channels) / retained[:, :, None]
    within = jnp.einsum('tsd,bsd->btd', matrix, scaled, precision=precise)
    back_re = power_real[:BLOCK][::-1]
    back_im = power_im[:BLOCK][::-1]
    end_re = weight[None] * jnp.einsum('bsd,sjd->bjd', scaled, back_re, precision=precise)
    end_im = weight[None] * jnp.einsum('bsd,sjd->bjd', scaled, back_im, precision=precise)
    closing = retained[:, -1][:, None, None]
    elements = (closing * power_real[BLOCK][None], closing * power_im[BLOCK][None], closing * end_re, closing * end_im)
    return (within, retained, elements, (power_real, power_im))

def ema_finish(within, retained, prior_re, prior_im, powers, ema_output, normed, ema_skip):
    power_real, power_im = powers
    multiplier_cosine_part = ema_output[0][None] * power_real[1:] - ema_output[1][None] * power_im[1:]
    coeff_im = ema_output[0][None] * power_im[1:] + ema_output[1][None] * power_real[1:]
    carried_part = jnp.einsum('bjd,tjd->btd', prior_re, multiplier_cosine_part, precision=precise) - jnp.einsum('bjd,tjd->btd', prior_im, coeff_im, precision=precise)
    mixed = retained[:, :, None] * (within + carried_part)
    return mixed.reshape(normed.shape) + ema_skip[None] * normed

def reference(tokens, retain, norm_gain, norm_bias, decay_rate, ema_angle, ema_input, ema_output, ema_skip, shared_weight, shared_gain, output_weight):
    width = D // N_TENSOR
    shards = (tokens.reshape(STREAM_LENGTH, N_TENSOR, width).transpose(1, 0, 2), norm_gain.reshape(N_TENSOR, width), norm_bias.reshape(N_TENSOR, width), decay_rate.reshape(NDIM, N_TENSOR, width).transpose(1, 0, 2), ema_angle.reshape(NDIM, N_TENSOR, width).transpose(1, 0, 2), ema_input.reshape(NDIM, N_TENSOR, width).transpose(1, 0, 2), ema_output.reshape(2, NDIM, N_TENSOR, width).transpose(2, 0, 1, 3), ema_skip.reshape(N_TENSOR, width), shared_weight.reshape(N_TENSOR, width, Z))

    def add_shard(running, shard):
        tokens_part, gain_part, bias_part, rate_part, angle_part, input_part, output_part, skip_part, weight_part = shard
        grouped, group_sums, group_squares = group_terms(tokens_part)
        before = jnp.zeros((2, group_sums.shape[1]), jnp.float32)
        normed = timestep_norm(grouped, group_sums, group_squares, before, jnp.zeros((), jnp.int32), gain_part, bias_part)
        within, retained, elements, powers = ema_local(normed, retain, rate_part, angle_part, input_part, output_part)
        inclusive = lax.associative_scan(block_combine, elements)
        prior_re = jnp.concatenate([jnp.zeros_like(inclusive[2][:1]), inclusive[2][:-1]], axis=0)
        prior_im = jnp.concatenate([jnp.zeros_like(inclusive[3][:1]), inclusive[3][:-1]], axis=0)
        ema = ema_finish(within, retained, prior_re, prior_im, powers, output_part, normed, skip_part)
        active = jax.nn.silu(ema).astype(jnp.bfloat16)
        term = jnp.dot(active, weight_part, preferred_element_type=jnp.float32).astype(jnp.bfloat16)
        term = lax.optimization_barrier(term).astype(jnp.float32)
        return (running + term, None)
    shared, unused = lax.scan(add_shard, jnp.zeros((STREAM_LENGTH, Z), jnp.float32), shards)
    squares = lax.optimization_barrier(jnp.mean(shared * shared, axis=1, keepdims=True))
    common_rescaled = (shared * lax.rsqrt(squares + scale_eps) * shared_gain[None]).astype(jnp.bfloat16)
    return jnp.dot(common_rescaled, output_weight, preferred_element_type=jnp.float32).astype(jnp.bfloat16)
```

```python
import functools

import jax
import jax.numpy as jnp
from jax import lax
from jax.experimental import pallas as pl
from jax.experimental.pallas import tpu as pltpu
from jax.sharding import PartitionSpec as P

GROUP = 64
STEPS = 8
NORM_EPS = 1e-05
SCALE_EPS = 1e-06

VMEM = pl.BlockSpec(memory_space=pltpu.VMEM)
SMEM = pl.BlockSpec(memory_space=pltpu.SMEM)


def dot(a, b):
    return jnp.dot(a, b, preferred_element_type=jnp.float32)


def pieces(values, count):
    out = []
    for _ in range(count):
        piece = values.astype(jnp.bfloat16)
        out.append(piece)
        values = values - piece.astype(jnp.float32)
    return out


def group_ones(channels):
    row = lax.broadcasted_iota(jnp.int32, (channels, channels), 0) // GROUP
    column = lax.broadcasted_iota(jnp.int32, (channels, channels), 1) // GROUP
    return (row == column).astype(jnp.bfloat16)


def stats_kernel(tokens_ref, retain_ref, stats_ref):
    length, channels = tokens_ref.shape
    values = tokens_ref[...].astype(jnp.float32)
    total = jnp.sum(values, axis=0, keepdims=True)
    squares = jnp.sum(values * values, axis=0, keepdims=True)
    rows = jnp.concatenate([total, squares, jnp.zeros((6, channels), jnp.float32)], axis=0)
    ones = group_ones(channels)
    grouped = sum(dot(piece, ones) for piece in pieces(rows, 3))
    kept = retain_ref[...]
    while kept.shape[0] > 1:
        half = kept.shape[0] // 2
        kept = kept[:half] * kept[half:]
    row = lax.broadcasted_iota(jnp.int32, (8, channels), 0)
    stats_ref[...] = jnp.where(row == 2, jnp.broadcast_to(kept, (8, channels)), grouped)


def span_stats(tokens, retain):
    return pl.pallas_call(
        stats_kernel,
        out_shape=jax.ShapeDtypeStruct((8, tokens.shape[1]), jnp.float32),
        in_specs=[VMEM, VMEM],
        out_specs=VMEM,
        name="span_stats",
    )(tokens, retain.reshape(-1, 1))


def local_kernel(tokens_ref, stats_ref, retain_ref, gain_ref, bias_ref, rate_ref, angle_ref, normed_ref, state_ref):
    length, channels = tokens_ref.shape
    ndim = rate_ref.shape[0]
    me = lax.axis_index("span")
    before = jnp.zeros((8, channels), jnp.float32)
    for other in range(stats_ref.shape[0]):
        before = before + jnp.where(other < me, stats_ref[other], 0.0)
    tokens = tokens_ref[...]
    values = tokens.astype(jnp.float32)
    ones = group_ones(channels)
    sums = dot(tokens, ones)
    squares = sum(dot(piece, ones) for piece in pieces(values * values, 2))
    row = lax.broadcasted_iota(jnp.int32, (length, length), 0)
    column = lax.broadcasted_iota(jnp.int32, (length, length), 1)
    lower = (column <= row).astype(jnp.bfloat16)
    cum_sum = before[0:1] + sum(dot(lower, piece) for piece in pieces(sums, 3))
    cum_sq = before[1:2] + sum(dot(lower, piece) for piece in pieces(squares, 3))
    position = lax.broadcasted_iota(jnp.int32, (length, channels), 0)
    counts = ((me * length + position + 1) * GROUP).astype(jnp.float32)
    average = cum_sum / counts
    spread = cum_sq / counts - average * average
    inverse = lax.rsqrt(spread + NORM_EPS)
    normed_ref[...] = (values - average) * inverse * gain_ref[...] + bias_ref[...]

    width = min(256, channels)
    for start in range(0, channels, width):
        lanes = slice(start, start + width)
        size = jnp.exp(-rate_ref[:, lanes])
        turn_re = size * jnp.cos(angle_ref[:, lanes])
        turn_im = size * jnp.sin(angle_ref[:, lanes])

        def steps(block, carried):
            re, im = carried
            first = pl.multiple_of(block * STEPS, STEPS)
            for step in range(STEPS):
                entry = normed_ref[pl.ds(first + step, 1), lanes]
                keep = retain_ref[first + step]
                re, im = (
                    (turn_re * re - turn_im * im) * keep + entry,
                    (turn_re * im + turn_im * re) * keep,
                )
            return re, im

        zero = jnp.zeros((ndim, width), jnp.float32)
        re, im = lax.fori_loop(0, length // STEPS, steps, (zero, zero))
        state_ref[0:ndim, lanes] = re.astype(state_ref.dtype)
        state_ref[ndim:, lanes] = im.astype(state_ref.dtype)


def local_scan(tokens, stats, retain, gain, bias, rate, angle):
    length, channels = tokens.shape
    return pl.pallas_call(
        local_kernel,
        out_shape=(
            jax.ShapeDtypeStruct((length, channels), jnp.float32),
            jax.ShapeDtypeStruct((2 * rate.shape[0], channels), jnp.bfloat16),
        ),
        in_specs=[VMEM, VMEM, SMEM, VMEM, VMEM, VMEM, VMEM],
        out_specs=(VMEM, VMEM),
        name="local_scan",
    )(tokens, stats, retain, gain.reshape(1, -1), bias.reshape(1, -1), rate, angle)


def full_kernel(normed_ref, states_ref, stats_ref, retain_ref, rate_ref, angle_ref, input_ref, output_ref, skip_ref, weight_ref, part_ref, ema_ref):
    length, channels = normed_ref.shape
    ndim = rate_ref.shape[0]
    me = lax.axis_index("span")
    width = min(256, channels)
    for start in range(0, channels, width):
        lanes = slice(start, start + width)
        rate, angle = rate_ref[:, lanes], angle_ref[:, lanes]
        size = jnp.exp(-rate)
        turn_re = size * jnp.cos(angle)
        turn_im = size * jnp.sin(angle)
        weight = (1.0 - size) * input_ref[:, lanes]
        read_re = weight * output_ref[0, :, lanes]
        read_im = weight * output_ref[1, :, lanes]
        whole = jnp.exp(-rate * length)
        whole_re = whole * jnp.cos(angle * length)
        whole_im = whole * jnp.sin(angle * length)
        re = jnp.zeros((ndim, width), jnp.float32)
        im = jnp.zeros((ndim, width), jnp.float32)
        for other in range(states_ref.shape[0]):
            keep = stats_ref[other, 2:3, lanes]
            here_re = states_ref[other, 0:ndim, lanes].astype(jnp.float32)
            here_im = states_ref[other, ndim:, lanes].astype(jnp.float32)
            next_re = (whole_re * re - whole_im * im) * keep + here_re
            next_im = (whole_re * im + whole_im * re) * keep + here_im
            re = jnp.where(other < me, next_re, re)
            im = jnp.where(other < me, next_im, im)

        def steps(block, carried):
            re, im = carried
            first = pl.multiple_of(block * STEPS, STEPS)
            for step in range(STEPS):
                entry = normed_ref[pl.ds(first + step, 1), lanes]
                keep = retain_ref[first + step]
                re, im = (
                    (turn_re * re - turn_im * im) * keep + entry,
                    (turn_re * im + turn_im * re) * keep,
                )
                ema_ref[pl.ds(first + step, 1), lanes] = jnp.sum(read_re * re - read_im * im, axis=0, keepdims=True)
            return re, im

        lax.fori_loop(0, length // STEPS, steps, (re, im))
    ema = ema_ref[...] + skip_ref[...] * normed_ref[...]
    active = (ema / (1.0 + jnp.exp(-ema))).astype(jnp.bfloat16)
    part_ref[...] = dot(active, weight_ref[...]).astype(jnp.bfloat16)


def full_scan(normed, states, stats, retain, rate, angle, source, output, skip, weight):
    length, channels = normed.shape
    return pl.pallas_call(
        full_kernel,
        out_shape=jax.ShapeDtypeStruct((length, weight.shape[1]), jnp.bfloat16),
        in_specs=[VMEM, VMEM, VMEM, SMEM] + [VMEM] * 6,
        out_specs=VMEM,
        scratch_shapes=[pltpu.VMEM((length, channels), jnp.float32)],
        name="full_scan",
    )(normed, states, stats, retain, rate, angle, source, output, skip.reshape(1, -1), weight)


def span_gather(values):
    return lax.all_gather(values, "span", axis=0)


def mix(part, gain):
    shared = lax.psum_scatter(part, "tensor", scatter_dimension=0, tiled=True).astype(jnp.float32)
    squares = jnp.mean(shared * shared, axis=1, keepdims=True)
    normed = (shared * lax.rsqrt(squares + SCALE_EPS) * gain[None]).astype(jnp.bfloat16)
    return lax.all_gather(normed, "tensor", axis=0, tiled=True)


def shards(tokens, retain, norm_gain, norm_bias, decay_rate, ema_angle, ema_input, ema_output, ema_skip, shared_weight, shared_gain, output_weight):
    stats = span_gather(span_stats(tokens, retain))
    normed, state = local_scan(tokens, stats, retain, norm_gain, norm_bias, decay_rate, ema_angle)
    states = span_gather(state)
    part = full_scan(normed, states, stats, retain, decay_rate, ema_angle, ema_input, ema_output, ema_skip, shared_weight)
    gathered = mix(part, shared_gain)
    return dot(gathered, output_weight).astype(jnp.bfloat16)


def solution(mesh):
    in_specs = (
        P("span", "tensor"),
        P("span"),
        P("tensor"),
        P("tensor"),
        P(None, "tensor"),
        P(None, "tensor"),
        P(None, "tensor"),
        P(None, None, "tensor"),
        P("tensor"),
        P("tensor", None),
        P(),
        P(None, "tensor"),
    )
    return jax.shard_map(shards, mesh=mesh, in_specs=in_specs, out_specs=P("span", "tensor"), check_vma=False)
```

```python
import functools

import jax
import jax.numpy as jnp
from jax import lax
from jax.experimental import pallas as pl
from jax.experimental.pallas import tpu as pltpu
from jax.sharding import PartitionSpec as P

GROUP = 64
STEPS = 8
KEPT = 16
NORM_EPS = 1e-05
SCALE_EPS = 1e-06

MESH = pl.DeviceIdType.MESH
VMEM = pl.BlockSpec(memory_space=pltpu.VMEM)
SMEM = pl.BlockSpec(memory_space=pltpu.SMEM)


def dot(a, b):
    return jnp.dot(a, b, preferred_element_type=jnp.float32)


def pieces(values, count):
    out = []
    for _ in range(count):
        piece = values.astype(jnp.bfloat16)
        out.append(piece)
        values = values - piece.astype(jnp.float32)
    return out


def group_ones(channels):
    row = lax.broadcasted_iota(jnp.int32, (channels, channels), 0) // GROUP
    column = lax.broadcasted_iota(jnp.int32, (channels, channels), 1) // GROUP
    return (row == column).astype(jnp.bfloat16)


def greet(axis, peers):
    barrier = pltpu.get_barrier_semaphore()
    for peer in peers:
        pl.semaphore_signal(barrier, inc=1, device_id={axis: peer}, device_id_type=MESH)
    pl.semaphore_wait(barrier, len(peers))


def spread_copies(source, landing, send_sem, recv_sem, count):
    me = lax.axis_index("span")
    copies = []
    for step in range(1, count):
        copy = pltpu.make_async_remote_copy(
            src_ref=source,
            dst_ref=landing.at[me],
            send_sem=send_sem.at[step - 1],
            recv_sem=recv_sem.at[step - 1],
            device_id={"span": lax.rem(me + step, count)},
            device_id_type=MESH,
        )
        copies.append(copy)
    return copies


def span_peers(count):
    me = lax.axis_index("span")
    return [lax.rem(me + step, count) for step in range(1, count)]


def stats_kernel(count, tokens_ref, stats_ref, own_ref, send_sem, recv_sem):
    length, channels = tokens_ref.shape
    me = lax.axis_index("span")
    values = tokens_ref[...].astype(jnp.float32)
    total = jnp.sum(values, axis=0, keepdims=True)
    squares = jnp.sum(values * values, axis=0, keepdims=True)
    rows = jnp.concatenate([total, squares, jnp.zeros((6, channels), jnp.float32)], axis=0)
    ones = group_ones(channels)
    own_ref[...] = sum(dot(piece, ones) for piece in pieces(rows, 3))
    greet("span", span_peers(count))
    copies = spread_copies(own_ref, stats_ref, send_sem, recv_sem, count)
    for copy in copies:
        copy.start()
    stats_ref[me] = own_ref[...]
    for copy in copies:
        copy.wait()


def span_stats(tokens):
    count = lax.axis_size("span")
    channels = tokens.shape[1]
    return pl.pallas_call(
        functools.partial(stats_kernel, count),
        out_shape=jax.ShapeDtypeStruct((count, 8, channels), jnp.float32),
        in_specs=[VMEM],
        out_specs=VMEM,
        scratch_shapes=[
            pltpu.VMEM((8, channels), jnp.float32),
            pltpu.SemaphoreType.DMA((count - 1,)),
            pltpu.SemaphoreType.DMA((count - 1,)),
        ],
        compiler_params=pltpu.CompilerParams(collective_id=0, has_side_effects=True),
        name="span_stats",
    )(tokens)


def gather_kernel(count, own_ref, all_ref, send_sem, recv_sem):
    me = lax.axis_index("span")
    greet("span", span_peers(count))
    copies = spread_copies(own_ref, all_ref, send_sem, recv_sem, count)
    for copy in copies:
        copy.start()
    all_ref[me] = own_ref[...]
    for copy in copies:
        copy.wait()


def span_gather(values):
    count = lax.axis_size("span")
    return pl.pallas_call(
        functools.partial(gather_kernel, count),
        out_shape=jax.ShapeDtypeStruct((count,) + values.shape, values.dtype),
        in_specs=[VMEM],
        out_specs=VMEM,
        scratch_shapes=[pltpu.SemaphoreType.DMA((count - 1,)), pltpu.SemaphoreType.DMA((count - 1,))],
        compiler_params=pltpu.CompilerParams(collective_id=1, has_side_effects=True),
        name="span_gather",
    )(values)


def local_kernel(tokens_ref, stats_ref, retain_ref, gain_ref, bias_ref, rate_ref, angle_ref, normed_ref, state_ref):
    length, channels = tokens_ref.shape
    ndim = rate_ref.shape[0]
    me = lax.axis_index("span")
    before = jnp.zeros((8, channels), jnp.float32)
    for other in range(stats_ref.shape[0]):
        before = before + jnp.where(other < me, stats_ref[other], 0.0)
    tokens = tokens_ref[...]
    values = tokens.astype(jnp.float32)
    ones = group_ones(channels)
    sums = dot(tokens, ones)
    squares = sum(dot(piece, ones) for piece in pieces(values * values, 2))
    row = lax.broadcasted_iota(jnp.int32, (length, length), 0)
    column = lax.broadcasted_iota(jnp.int32, (length, length), 1)
    lower = (column <= row).astype(jnp.bfloat16)
    cum_sum = before[0:1] + sum(dot(lower, piece) for piece in pieces(sums, 3))
    cum_sq = before[1:2] + sum(dot(lower, piece) for piece in pieces(squares, 3))
    position = lax.broadcasted_iota(jnp.int32, (length, channels), 0)
    counts = ((me * length + position + 1) * GROUP).astype(jnp.float32)
    average = cum_sum / counts
    spread = cum_sq / counts - average * average
    inverse = lax.rsqrt(spread + NORM_EPS)
    normed_ref[...] = (values - average) * inverse * gain_ref[...] + bias_ref[...]

    width = min(256, channels)
    for start in range(0, channels, width):
        lanes = slice(start, start + width)
        size = jnp.exp(-rate_ref[:, lanes])
        turn_re = size * jnp.cos(angle_ref[:, lanes])
        turn_im = size * jnp.sin(angle_ref[:, lanes])

        def steps(block, carried):
            re, im, kept = carried
            first = pl.multiple_of(block * STEPS, STEPS)
            for step in range(STEPS):
                entry = normed_ref[pl.ds(first + step, 1), lanes]
                keep = retain_ref[first + step]
                kept = kept * keep
                re, im = (
                    (turn_re * re - turn_im * im) * keep + entry,
                    (turn_re * im + turn_im * re) * keep,
                )
            return re, im, kept

        zero = jnp.zeros((ndim, width), jnp.float32)
        re, im, kept = lax.fori_loop(0, length // STEPS, steps, (zero, zero, jnp.float32(1.0)))
        state_ref[0:ndim, lanes] = re.astype(state_ref.dtype)
        state_ref[ndim : 2 * ndim, lanes] = im.astype(state_ref.dtype)
        high, middle, low = pieces(jnp.full((KEPT, width), kept, jnp.float32), 3)
        row = lax.broadcasted_iota(jnp.int32, (KEPT, width), 0)
        rest = jnp.where(row == 1, middle.astype(jnp.float32), low.astype(jnp.float32))
        state_ref[2 * ndim :, lanes] = jnp.where(row == 0, high.astype(jnp.float32), rest).astype(state_ref.dtype)


def local_scan(tokens, stats, retain, gain, bias, rate, angle):
    length, channels = tokens.shape
    return pl.pallas_call(
        local_kernel,
        out_shape=(
            jax.ShapeDtypeStruct((length, channels), jnp.float32),
            jax.ShapeDtypeStruct((2 * rate.shape[0] + KEPT, channels), jnp.bfloat16),
        ),
        in_specs=[VMEM, VMEM, SMEM, VMEM, VMEM, VMEM, VMEM],
        out_specs=(VMEM, VMEM),
        name="local_scan",
    )(tokens, stats, retain, gain.reshape(1, -1), bias.reshape(1, -1), rate, angle)


def full_kernel(normed_ref, states_ref, retain_ref, rate_ref, angle_ref, input_ref, output_ref, skip_ref, weight_ref, part_ref, ema_ref):
    length, channels = normed_ref.shape
    ndim = rate_ref.shape[0]
    me = lax.axis_index("span")
    width = min(256, channels)
    for start in range(0, channels, width):
        lanes = slice(start, start + width)
        rate, angle = rate_ref[:, lanes], angle_ref[:, lanes]
        size = jnp.exp(-rate)
        turn_re = size * jnp.cos(angle)
        turn_im = size * jnp.sin(angle)
        weight = (1.0 - size) * input_ref[:, lanes]
        read_re = weight * output_ref[0, :, lanes]
        read_im = weight * output_ref[1, :, lanes]
        whole = jnp.exp(-rate * length)
        whole_re = whole * jnp.cos(angle * length)
        whole_im = whole * jnp.sin(angle * length)
        re = jnp.zeros((ndim, width), jnp.float32)
        im = jnp.zeros((ndim, width), jnp.float32)
        for other in range(states_ref.shape[0]):
            kept = states_ref[other, 2 * ndim :, lanes].astype(jnp.float32)
            keep = kept[0:1] + kept[1:2] + kept[2:3]
            here_re = states_ref[other, 0:ndim, lanes].astype(jnp.float32)
            here_im = states_ref[other, ndim : 2 * ndim, lanes].astype(jnp.float32)
            next_re = (whole_re * re - whole_im * im) * keep + here_re
            next_im = (whole_re * im + whole_im * re) * keep + here_im
            re = jnp.where(other < me, next_re, re)
            im = jnp.where(other < me, next_im, im)

        def steps(block, carried):
            re, im = carried
            first = pl.multiple_of(block * STEPS, STEPS)
            for step in range(STEPS):
                entry = normed_ref[pl.ds(first + step, 1), lanes]
                keep = retain_ref[first + step]
                re, im = (
                    (turn_re * re - turn_im * im) * keep + entry,
                    (turn_re * im + turn_im * re) * keep,
                )
                ema_ref[pl.ds(first + step, 1), lanes] = jnp.sum(read_re * re - read_im * im, axis=0, keepdims=True)
            return re, im

        lax.fori_loop(0, length // STEPS, steps, (re, im))
    ema = ema_ref[...] + skip_ref[...] * normed_ref[...]
    active = (ema / (1.0 + jnp.exp(-ema))).astype(jnp.bfloat16)
    part_ref[...] = dot(active, weight_ref[...]).astype(jnp.bfloat16)


def full_scan(normed, states, retain, rate, angle, source, output, skip, weight):
    length, channels = normed.shape
    return pl.pallas_call(
        full_kernel,
        out_shape=jax.ShapeDtypeStruct((length, weight.shape[1]), jnp.bfloat16),
        in_specs=[VMEM, VMEM, SMEM] + [VMEM] * 6,
        out_specs=VMEM,
        scratch_shapes=[pltpu.VMEM((length, channels), jnp.float32)],
        name="full_scan",
    )(normed, states, retain, rate, angle, source, output, skip.reshape(1, -1), weight)


def mix_kernel(chips, part_ref, gain_ref, out_ref, near_ref, sum_ref, far_ref, own_ref, pair_send, pair_recv, far_send, far_recv, out_send, out_recv, back_send, back_recv):
    me = lax.axis_index("tensor")
    core = lax.rem(me, 2)
    chip = lax.div(me, 2)
    partner = me + 1 - 2 * core
    order = [lax.rem(chip + step, chips) for step in range(1, chips)] + [chip]
    peers = [2 * place + core for place in order[:-1]]
    greet("tensor", [partner] + peers)

    def send(source, target, send_sem, recv_sem, device):
        return pltpu.make_async_remote_copy(
            src_ref=source,
            dst_ref=target,
            send_sem=send_sem,
            recv_sem=recv_sem,
            device_id={"tensor": device},
            device_id_type=MESH,
        )

    pair = []
    for slot, place in enumerate(order):
        copy = send(part_ref.at[place, 1 - core], near_ref.at[slot], pair_send.at[slot], pair_recv.at[slot], partner)
        copy.start()
        pair.append(copy)
    far = []
    for slot, place in enumerate(order[:-1]):
        pair[slot].wait_recv()
        added = part_ref[place, core].astype(jnp.float32) + near_ref[slot].astype(jnp.float32)
        sum_ref[slot] = added.astype(jnp.bfloat16)
        copy = send(sum_ref.at[slot], far_ref.at[slot], far_send.at[slot], far_recv.at[slot], peers[slot])
        copy.start()
        far.append(copy)
    pair[-1].wait_recv()
    shared = part_ref[chip, core].astype(jnp.float32) + near_ref[chips - 1].astype(jnp.float32)
    for slot in range(chips - 1):
        far[slot].wait_recv()
        shared = shared + far_ref[slot].astype(jnp.float32)
    squares = jnp.mean(shared * shared, axis=1, keepdims=True)
    own_ref[...] = (shared * lax.rsqrt(squares + SCALE_EPS) * gain_ref[...]).astype(jnp.bfloat16)
    outward = []
    for slot in range(chips - 1):
        copy = send(own_ref, out_ref.at[chip, core], out_send.at[slot], out_recv.at[slot], peers[slot])
        copy.start()
        outward.append(copy)
    back = [send(own_ref, out_ref.at[chip, core], back_send.at[chips - 1], back_recv.at[chips - 1], partner)]
    back[0].start()
    out_ref[chip, core] = own_ref[...]
    for slot in range(chips - 1):
        origin = lax.rem(chip + chips - 1 - slot, chips)
        outward[slot].wait_recv()
        block = out_ref.at[origin, core]
        copy = send(block, block, back_send.at[slot], back_recv.at[slot], partner)
        copy.start()
        back.append(copy)
    for copy in back:
        copy.wait()
    for copy in pair + far + outward:
        copy.wait_send()


def mix(part, gain):
    chips = lax.axis_size("tensor") // 2
    rows, columns = part.shape[0] // (2 * chips), part.shape[1]
    block = (rows, columns)
    gathered = pl.pallas_call(
        functools.partial(mix_kernel, chips),
        out_shape=jax.ShapeDtypeStruct((chips, 2) + block, jnp.bfloat16),
        in_specs=[VMEM, VMEM],
        out_specs=VMEM,
        scratch_shapes=[
            pltpu.VMEM((chips,) + block, jnp.bfloat16),
            pltpu.VMEM((chips - 1,) + block, jnp.bfloat16),
            pltpu.VMEM((chips - 1,) + block, jnp.bfloat16),
            pltpu.VMEM(block, jnp.bfloat16),
            pltpu.SemaphoreType.DMA((chips,)),
            pltpu.SemaphoreType.DMA((chips,)),
            pltpu.SemaphoreType.DMA((chips - 1,)),
            pltpu.SemaphoreType.DMA((chips - 1,)),
            pltpu.SemaphoreType.DMA((chips - 1,)),
            pltpu.SemaphoreType.DMA((chips - 1,)),
            pltpu.SemaphoreType.DMA((chips,)),
            pltpu.SemaphoreType.DMA((chips,)),
        ],
        compiler_params=pltpu.CompilerParams(collective_id=2, has_side_effects=True),
        name="mix",
    )(part.reshape((chips, 2) + block), gain.reshape(1, -1))
    return gathered.reshape(part.shape)


def shards(tokens, retain, norm_gain, norm_bias, decay_rate, ema_angle, ema_input, ema_output, ema_skip, shared_weight, shared_gain, output_weight):
    stats = span_stats(tokens)
    normed, state = local_scan(tokens, stats, retain, norm_gain, norm_bias, decay_rate, ema_angle)
    states = span_gather(state)
    part = full_scan(normed, states, retain, decay_rate, ema_angle, ema_input, ema_output, ema_skip, shared_weight)
    gathered = mix(part, shared_gain)
    return dot(gathered, output_weight).astype(jnp.bfloat16)


def solution(mesh):
    in_specs = (
        P("span", "tensor"),
        P("span"),
        P("tensor"),
        P("tensor"),
        P(None, "tensor"),
        P(None, "tensor"),
        P(None, "tensor"),
        P(None, None, "tensor"),
        P("tensor"),
        P("tensor", None),
        P(),
        P(None, "tensor"),
    )
    return jax.shard_map(shards, mesh=mesh, in_specs=in_specs, out_specs=P("span", "tensor"), check_vma=False)
```

```python
import functools

import jax
import jax.numpy as jnp
from jax import lax
from jax.experimental import pallas as pl
from jax.experimental.pallas import tpu as pltpu
from jax.sharding import PartitionSpec as P

GROUP = 64
STEPS = 8
LANES = 128
NORM_EPS = 1e-05
SCALE_EPS = 1e-06

MESH = pl.DeviceIdType.MESH
VMEM = pl.BlockSpec(memory_space=pltpu.VMEM)


def dot(a, b):
    return jnp.dot(a, b, preferred_element_type=jnp.float32)


def pieces(values, count):
    out = []
    for _ in range(count):
        piece = values.astype(jnp.bfloat16)
        out.append(piece)
        values = values - piece.astype(jnp.float32)
    return out


def group_ones(channels):
    row = lax.broadcasted_iota(jnp.int32, (channels, channels), 0) // GROUP
    column = lax.broadcasted_iota(jnp.int32, (channels, channels), 1) // GROUP
    return (row == column).astype(jnp.bfloat16)


def remote(source, target, send_sem, recv_sem, axis, device):
    return pltpu.make_async_remote_copy(
        src_ref=source,
        dst_ref=target,
        send_sem=send_sem,
        recv_sem=recv_sem,
        device_id={axis: device},
        device_id_type=MESH,
    )


def to_later(count, pairs, send_sem, recv_sem):
    me = lax.axis_index("span")
    for step in range(1, count):

        @pl.when(me + step < count)
        def _():
            for item, (source, landing) in enumerate(pairs):
                remote(source, landing.at[me], send_sem.at[item, step - 1], recv_sem.at[item, step - 1], "span", me + step).start()


def from_earlier(count, pairs, send_sem, recv_sem):
    me = lax.axis_index("span")
    for step in range(1, count):

        @pl.when(me >= step)
        def _():
            for item, (source, landing) in enumerate(pairs):
                remote(source, landing.at[me], send_sem.at[item, step - 1], recv_sem.at[item, step - 1], "span", me - step).wait_recv()

        @pl.when(me + step < count)
        def _():
            for item, (source, landing) in enumerate(pairs):
                remote(source, landing.at[me], send_sem.at[item, step - 1], recv_sem.at[item, step - 1], "span", me + step).wait_send()


def wide(column, width):
    return jnp.concatenate([column] * (width // LANES), axis=1)


def lanes_of(channels, width):
    return [slice(start, start + width) for start in range(0, channels, width)]


def layer_kernel(
    count,
    chips,
    tokens_ref,
    retain_ref,
    norm_gain_ref,
    bias_ref,
    rate_ref,
    angle_ref,
    input_ref,
    output_ref,
    skip_ref,
    gain_ref,
    weight_hbm,
    mixer_hbm,
    out_ref,
    weight_ref,
    mixer_ref,
    total_ref,
    totals_ref,
    before_ref,
    normed_ref,
    scaled_ref,
    prefix_ref,
    power_ref,
    unit_ref,
    read_ref,
    start_ref,
    state_ref,
    states_ref,
    kept_ref,
    kepts_ref,
    ema_ref,
    part_ref,
    near_ref,
    sum_ref,
    far_ref,
    own_ref,
    all_ref,
    load_sem,
    total_send,
    total_recv,
    state_send,
    state_recv,
    pair_send,
    pair_recv,
    far_send,
    far_recv,
    out_send,
    out_recv,
    back_send,
    back_recv,
):
    length, channels = tokens_ref.shape
    ndim = rate_ref.shape[0]
    blocks = length // STEPS
    rows = part_ref.shape[2]
    span = lax.axis_index("span")
    me = lax.axis_index("tensor")
    core = lax.rem(me, 2)
    chip = lax.div(me, 2)
    partner = me + 1 - 2 * core
    order = [lax.rem(chip + step, chips) for step in range(1, chips)] + [chip]
    peers = [2 * place + core for place in order[:-1]]

    barrier = pltpu.get_barrier_semaphore()
    for step in range(1, count):
        pl.semaphore_signal(barrier, inc=1, device_id={"span": lax.rem(span + step, count)}, device_id_type=MESH)
    for peer in [partner] + peers:
        pl.semaphore_signal(barrier, inc=1, device_id={"tensor": peer}, device_id_type=MESH)
    loads = [
        pltpu.make_async_copy(weight_hbm, weight_ref, load_sem.at[0]),
        pltpu.make_async_copy(mixer_hbm, mixer_ref, load_sem.at[1]),
    ]
    for load in loads:
        load.start()

    tokens = tokens_ref[...]
    values = tokens.astype(jnp.float32)
    ones = group_ones(channels)
    total = jnp.sum(values, axis=0, keepdims=True)
    squares = jnp.sum(values * values, axis=0, keepdims=True)
    summed = jnp.concatenate([total, squares, jnp.zeros((6, channels), jnp.float32)], axis=0)
    total_ref[...] = sum(dot(piece, ones) for piece in pieces(summed, 3))
    pl.semaphore_wait(barrier, count - 1 + chips)
    stats_pairs = [(total_ref, totals_ref)]
    to_later(count, stats_pairs, total_send, total_recv)

    rate, angle = rate_ref[...], angle_ref[...]
    size = jnp.exp(-rate)
    turn_re = size * jnp.cos(angle)
    turn_im = size * jnp.sin(angle)
    weight = (1.0 - size) * input_ref[...]
    read_re = weight * output_ref[0]
    read_im = weight * output_ref[1]
    power_re, power_im = jnp.ones_like(rate), jnp.zeros_like(rate)
    lag_rows = []
    for lag in range(STEPS + 1):
        if lag < STEPS:
            lag_rows.append(jnp.sum(read_re * power_re - read_im * power_im, axis=0, keepdims=True))
        power_ref[0, lag] = power_re
        power_ref[1, lag] = power_im
        power_re, power_im = power_re * turn_re - power_im * turn_im, power_re * turn_im + power_im * turn_re
    unit_ref[0] = read_re * turn_re - read_im * turn_im
    unit_ref[1] = read_re * turn_im + read_im * turn_re
    step_row = lax.broadcasted_iota(jnp.int32, (STEPS, channels), 0)

    def table(part, carried):
        here = pl.ds(part, 1)
        re = jnp.broadcast_to(unit_ref[0, here, :], (STEPS, channels))
        im = jnp.broadcast_to(unit_ref[1, here, :], (STEPS, channels))
        for bit in (1, 2, 4):
            chosen = (step_row // bit) % 2 == 1
            by_re = jnp.where(chosen, jnp.broadcast_to(power_ref[0, bit, here, :], (STEPS, channels)), 1.0)
            by_im = jnp.where(chosen, jnp.broadcast_to(power_ref[1, bit, here, :], (STEPS, channels)), 0.0)
            re, im = re * by_re - im * by_im, re * by_im + im * by_re
        read_ref[0, part] = re
        read_ref[1, part] = im
        return carried

    lax.fori_loop(0, ndim, table, 0)

    sums = dot(tokens, ones)
    squares = sum(dot(piece, ones) for piece in pieces(values * values, 2))
    row = lax.broadcasted_iota(jnp.int32, (length, length), 0)
    column = lax.broadcasted_iota(jnp.int32, (length, length), 1)
    lower = (column <= row).astype(jnp.bfloat16)
    cum_sum = sum(dot(lower, piece) for piece in pieces(sums, 3))
    cum_sq = sum(dot(lower, piece) for piece in pieces(squares, 3))
    diagonal = jnp.where(row == column, jnp.broadcast_to(retain_ref[...], (length, length)), 0.0)
    keep = sum(dot(piece, jnp.ones((length, LANES), jnp.bfloat16)) for piece in pieces(diagonal, 3))
    place_in = lax.broadcasted_iota(jnp.int32, (length, LANES), 0) % STEPS
    prefix = keep
    suffix = jnp.where(place_in < STEPS - 1, pltpu.roll(keep, length - 1, 0), 1.0)
    for by in (1, 2, 4):
        prefix = jnp.where(place_in >= by, prefix * pltpu.roll(prefix, by, 0), prefix)
        suffix = jnp.where(place_in + by < STEPS, suffix * pltpu.roll(suffix, length - by, 0), suffix)
    prefix_ref[...] = prefix
    position = lax.broadcasted_iota(jnp.int32, (length, channels), 0)
    counts = ((span * length + position + 1) * GROUP).astype(jnp.float32)

    from_earlier(count, stats_pairs, total_send, total_recv)
    before_ref[...] = jnp.zeros((8, channels), jnp.float32)
    for other in range(count - 1):

        @pl.when(other < span)
        def _():
            before_ref[...] += totals_ref[other]

    average = (before_ref[0:1] + cum_sum) / counts
    spread = (before_ref[1:2] + cum_sq) / counts - average * average
    inverse = lax.rsqrt(spread + NORM_EPS)
    normed = (values - average) * inverse * norm_gain_ref[...] + bias_ref[...]
    normed_ref[...] = normed
    scaled_ref[...] = normed * wide(suffix, channels)

    width = min(256, channels)
    for lanes in lanes_of(channels, width):
        whole_re, whole_im = power_ref[0, STEPS, :, lanes], power_ref[1, STEPS, :, lanes]

        def enter(block, carried):
            re, im, kept = carried
            start_ref[0, block, :, lanes] = re
            start_ref[1, block, :, lanes] = im
            first = pl.multiple_of(block * STEPS, STEPS)
            factor = wide(prefix_ref[pl.ds(first + STEPS - 1, 1), :], width)
            next_re = (whole_re * re - whole_im * im) * factor
            next_im = (whole_re * im + whole_im * re) * factor
            for step in range(STEPS):
                entry = scaled_ref[pl.ds(first + step, 1), lanes]
                lag = STEPS - 1 - step
                if lag:
                    next_re = next_re + power_ref[0, lag, :, lanes] * entry
                    next_im = next_im + power_ref[1, lag, :, lanes] * entry
                else:
                    next_re = next_re + entry
            return next_re, next_im, kept * factor

        zero = jnp.zeros((ndim, width), jnp.float32)
        re, im, kept = lax.fori_loop(0, blocks, enter, (zero, zero, jnp.ones((1, width), jnp.float32)))
        state_ref[0:ndim, lanes] = re.astype(state_ref.dtype)
        state_ref[ndim : 2 * ndim, lanes] = im.astype(state_ref.dtype)
    kept_ref[...] = jnp.broadcast_to(kept[:, :LANES], (8, LANES))
    state_pairs = [(state_ref, states_ref), (kept_ref, kepts_ref)]
    to_later(count, state_pairs, state_send, state_recv)

    for lanes in lanes_of(channels, LANES):
        reach = jnp.where(place_in >= 0, 1.0, 0.0)
        here = normed_ref[:, lanes]
        within = here * lag_rows[0][:, lanes]
        for lag in range(1, STEPS):
            reach = jnp.where(place_in >= lag, reach * (pltpu.roll(keep, lag - 1, 0) if lag > 1 else keep), 0.0)
            within = within + pltpu.roll(here, lag, 0) * (lag_rows[lag][:, lanes] * reach)
        ema_ref[:, lanes] = within + skip_ref[:, lanes] * here

    from_earlier(count, state_pairs, state_send, state_recv)
    whole = jnp.exp(-rate * length)
    unit_ref[0] = whole * jnp.cos(angle * length)
    unit_ref[1] = whole * jnp.sin(angle * length)
    power_ref[0, 0] = jnp.zeros_like(rate)
    power_ref[1, 0] = jnp.zeros_like(rate)
    for other in range(count - 1):

        @pl.when(other < span)
        def _():
            kept = wide(kepts_ref[other, 0:1, :], channels)
            re, im = power_ref[0, 0], power_ref[1, 0]
            by_re, by_im = unit_ref[0], unit_ref[1]
            power_ref[0, 0] = (by_re * re - by_im * im) * kept + states_ref[other, 0:ndim].astype(jnp.float32)
            power_ref[1, 0] = (by_re * im + by_im * re) * kept + states_ref[other, ndim : 2 * ndim].astype(jnp.float32)

    for lanes in lanes_of(channels, width):
        whole_re, whole_im = power_ref[0, STEPS, :, lanes], power_ref[1, STEPS, :, lanes]

        def arrive(block, carried):
            re, im = carried
            start_ref[0, block, :, lanes] += re
            start_ref[1, block, :, lanes] += im
            factor = wide(prefix_ref[pl.ds(block * STEPS + STEPS - 1, 1), :], width)
            return (whole_re * re - whole_im * im) * factor, (whole_re * im + whole_im * re) * factor

        lax.fori_loop(0, blocks, arrive, (power_ref[0, 0, :, lanes], power_ref[1, 0, :, lanes]))

        def leave(block, carried):
            first = pl.multiple_of(block * STEPS, STEPS)
            parts = [jnp.zeros((STEPS, width), jnp.float32) for _ in range(4)]
            for part in range(ndim):
                here = pl.ds(part, 1)
                slot = 2 * (part % 2)
                parts[slot] = parts[slot] + read_ref[0, part, :, lanes] * start_ref[0, block, here, lanes]
                parts[slot + 1] = parts[slot + 1] + read_ref[1, part, :, lanes] * start_ref[1, block, here, lanes]
            read = (parts[0] - parts[1]) + (parts[2] - parts[3])
            ema_ref[pl.ds(first, STEPS), lanes] += read * wide(prefix_ref[pl.ds(first, STEPS), :], width)
            return carried

        lax.fori_loop(0, blocks, leave, 0)

    ema = ema_ref[...]
    active = (ema / (1.0 + jnp.exp(-ema))).astype(jnp.bfloat16)
    for load in loads:
        load.wait()
    product = dot(active, weight_ref[...]).astype(jnp.bfloat16)
    part_ref[...] = product.reshape(part_ref.shape)

    pair = []
    for slot, place in enumerate(order):
        copy = remote(part_ref.at[place, 1 - core], near_ref.at[slot], pair_send.at[slot], pair_recv.at[slot], "tensor", partner)
        copy.start()
        pair.append(copy)
    far = []
    for slot, place in enumerate(order[:-1]):
        pair[slot].wait_recv()
        added = part_ref[place, core].astype(jnp.float32) + near_ref[slot].astype(jnp.float32)
        sum_ref[slot] = added.astype(jnp.bfloat16)
        copy = remote(sum_ref.at[slot], far_ref.at[slot], far_send.at[slot], far_recv.at[slot], "tensor", peers[slot])
        copy.start()
        far.append(copy)
    pair[-1].wait_recv()
    shared = part_ref[chip, core].astype(jnp.float32) + near_ref[chips - 1].astype(jnp.float32)
    for slot in range(chips - 1):
        far[slot].wait_recv()
        shared = shared + far_ref[slot].astype(jnp.float32)
    squares = jnp.mean(shared * shared, axis=1, keepdims=True)
    own_ref[...] = (shared * lax.rsqrt(squares + SCALE_EPS) * gain_ref[...]).astype(jnp.bfloat16)
    outward = []
    for slot in range(chips - 1):
        copy = remote(own_ref, all_ref.at[chip, core], out_send.at[slot], out_recv.at[slot], "tensor", peers[slot])
        copy.start()
        outward.append(copy)
    home = remote(own_ref, all_ref.at[chip, core], back_send.at[chips - 1], back_recv.at[chips - 1], "tensor", partner)
    home.start()
    all_ref[chip, core] = own_ref[...]
    columns = all_ref.shape[3]

    def finish(place):
        gathered = all_ref[place].reshape(2 * rows, columns)
        out_ref[place] = dot(gathered, mixer_ref[...]).astype(jnp.bfloat16)

    home.wait_recv()
    finish(chip)
    back = []
    for slot in range(chips - 1):
        origin = lax.rem(chip + chips - 1 - slot, chips)
        outward[slot].wait_recv()
        block = all_ref.at[origin, core]
        copy = remote(block, block, back_send.at[slot], back_recv.at[slot], "tensor", partner)
        copy.start()
        back.append(copy)
        if slot:
            back[slot - 1].wait_recv()
            finish(lax.rem(chip + chips - slot, chips))
    back[-1].wait_recv()
    finish(lax.rem(chip + 1, chips))
    for copy in pair + far + outward + back + [home]:
        copy.wait_send()


def layer(tokens, retain, norm_gain, norm_bias, rate, angle, source, output, skip, weight, gain, mixer):
    length, channels = tokens.shape
    ndim = rate.shape[0]
    blocks = length // STEPS
    count = lax.axis_size("span")
    chips = lax.axis_size("tensor") // 2
    rows, columns = length // (2 * chips), weight.shape[1]
    block = (rows, columns)
    f32, bf16 = jnp.float32, jnp.bfloat16
    sems = pltpu.SemaphoreType.DMA
    hbm = pl.BlockSpec(memory_space=pltpu.HBM)
    out = pl.pallas_call(
        functools.partial(layer_kernel, count, chips),
        out_shape=jax.ShapeDtypeStruct((chips, 2 * rows, mixer.shape[1]), bf16),
        in_specs=[VMEM] * 10 + [hbm, hbm],
        out_specs=VMEM,
        scratch_shapes=[
            pltpu.VMEM(weight.shape, bf16),
            pltpu.VMEM(mixer.shape, bf16),
            pltpu.VMEM((8, channels), f32),
            pltpu.VMEM((count, 8, channels), f32),
            pltpu.VMEM((8, channels), f32),
            pltpu.VMEM((length, channels), f32),
            pltpu.VMEM((length, channels), f32),
            pltpu.VMEM((length, LANES), f32),
            pltpu.VMEM((2, STEPS + 1, ndim, channels), f32),
            pltpu.VMEM((2, ndim, channels), f32),
            pltpu.VMEM((2, ndim, STEPS, channels), f32),
            pltpu.VMEM((2, blocks, ndim, channels), f32),
            pltpu.VMEM((2 * ndim, channels), bf16),
            pltpu.VMEM((count, 2 * ndim, channels), bf16),
            pltpu.VMEM((8, LANES), f32),
            pltpu.VMEM((count, 8, LANES), f32),
            pltpu.VMEM((length, channels), f32),
            pltpu.VMEM((chips, 2) + block, bf16),
            pltpu.VMEM((chips,) + block, bf16),
            pltpu.VMEM((chips - 1,) + block, bf16),
            pltpu.VMEM((chips - 1,) + block, bf16),
            pltpu.VMEM(block, bf16),
            pltpu.VMEM((chips, 2) + block, bf16),
            sems((2,)),
            sems((1, count - 1)),
            sems((1, count - 1)),
            sems((2, count - 1)),
            sems((2, count - 1)),
            sems((chips,)),
            sems((chips,)),
            sems((chips - 1,)),
            sems((chips - 1,)),
            sems((chips - 1,)),
            sems((chips - 1,)),
            sems((chips,)),
            sems((chips,)),
        ],
        compiler_params=pltpu.CompilerParams(collective_id=0, has_side_effects=True, vmem_limit_bytes=40 << 20),
        name="layer",
    )(
        tokens,
        retain.reshape(1, -1),
        norm_gain.reshape(1, -1),
        norm_bias.reshape(1, -1),
        rate,
        angle,
        source,
        output,
        skip.reshape(1, -1),
        gain.reshape(1, -1),
        weight,
        mixer,
    )
    return out.reshape(length, mixer.shape[1])


def solution(mesh):
    in_specs = (
        P("span", "tensor"),
        P("span"),
        P("tensor"),
        P("tensor"),
        P(None, "tensor"),
        P(None, "tensor"),
        P(None, "tensor"),
        P(None, None, "tensor"),
        P("tensor"),
        P("tensor", None),
        P(),
        P(None, "tensor"),
    )
    return jax.shard_map(layer, mesh=mesh, in_specs=in_specs, out_specs=P("span", "tensor"), check_vma=False)
```

```python
import functools

import jax
import jax.numpy as jnp
from jax import lax
from jax.experimental import pallas as pl
from jax.experimental.pallas import tpu as pltpu
from jax.sharding import PartitionSpec as P

GROUP = 64
STEPS = 8
LANES = 128
NORM_EPS = 1e-05
SCALE_EPS = 1e-06

MESH = pl.DeviceIdType.MESH
VMEM = pl.BlockSpec(memory_space=pltpu.VMEM)


def dot(a, b):
    return jnp.dot(a, b, preferred_element_type=jnp.float32)


def pieces(values, count):
    out = []
    for _ in range(count):
        piece = values.astype(jnp.bfloat16)
        out.append(piece)
        values = values - piece.astype(jnp.float32)
    return out


def group_ones(channels):
    row = lax.broadcasted_iota(jnp.int32, (channels, channels), 0) // GROUP
    column = lax.broadcasted_iota(jnp.int32, (channels, channels), 1) // GROUP
    return (row == column).astype(jnp.bfloat16)


def remote(source, target, send_sem, recv_sem, axis, device):
    return pltpu.make_async_remote_copy(
        src_ref=source,
        dst_ref=target,
        send_sem=send_sem,
        recv_sem=recv_sem,
        device_id={axis: device},
        device_id_type=MESH,
    )


def to_later(count, pairs, send_sem, recv_sem):
    me = lax.axis_index("span")
    for step in range(1, count):

        @pl.when(me + step < count)
        def _():
            for item, (source, landing) in enumerate(pairs):
                remote(source, landing.at[me], send_sem.at[item, step - 1], recv_sem.at[item, step - 1], "span", me + step).start()


def from_earlier(count, pairs, send_sem, recv_sem):
    me = lax.axis_index("span")
    for step in range(1, count):

        @pl.when(me >= step)
        def _():
            for item, (source, landing) in enumerate(pairs):
                remote(source, landing.at[me], send_sem.at[item, step - 1], recv_sem.at[item, step - 1], "span", me - step).wait_recv()

        @pl.when(me + step < count)
        def _():
            for item, (source, landing) in enumerate(pairs):
                remote(source, landing.at[me], send_sem.at[item, step - 1], recv_sem.at[item, step - 1], "span", me + step).wait_send()


def wide(column, width):
    return jnp.concatenate([column] * (width // LANES), axis=1)


def lanes_of(channels, width):
    return [slice(start, start + width) for start in range(0, channels, width)]


def layer_kernel(
    count,
    chips,
    tokens_ref,
    retain_ref,
    norm_gain_ref,
    bias_ref,
    rate_ref,
    angle_ref,
    input_ref,
    output_ref,
    skip_ref,
    gain_ref,
    weight_hbm,
    mixer_hbm,
    out_ref,
    weight_ref,
    mixer_ref,
    total_ref,
    totals_ref,
    before_ref,
    normed_ref,
    scaled_ref,
    prefix_ref,
    power_ref,
    unit_ref,
    read_ref,
    start_ref,
    state_ref,
    states_ref,
    kept_ref,
    kepts_ref,
    ema_ref,
    part_ref,
    near_ref,
    sum_ref,
    far_ref,
    own_ref,
    all_ref,
    load_sem,
    total_send,
    total_recv,
    state_send,
    state_recv,
    pair_send,
    pair_recv,
    far_send,
    far_recv,
    out_send,
    out_recv,
    back_send,
    back_recv,
):
    length, channels = tokens_ref.shape
    ndim = rate_ref.shape[0]
    blocks = length // STEPS
    halves, rows = part_ref.shape[2:4]
    span = lax.axis_index("span")
    me = lax.axis_index("tensor")
    core = lax.rem(me, 2)
    chip = lax.div(me, 2)
    partner = me + 1 - 2 * core
    order = [lax.rem(chip + step, chips) for step in range(1, chips)] + [chip]
    peers = [2 * place + core for place in order[:-1]]

    barrier = pltpu.get_barrier_semaphore()
    for step in range(1, count):
        pl.semaphore_signal(barrier, inc=1, device_id={"span": lax.rem(span + step, count)}, device_id_type=MESH)
    for peer in [partner] + peers:
        pl.semaphore_signal(barrier, inc=1, device_id={"tensor": peer}, device_id_type=MESH)
    loads = [
        pltpu.make_async_copy(weight_hbm, weight_ref, load_sem.at[0]),
        pltpu.make_async_copy(mixer_hbm, mixer_ref, load_sem.at[1]),
    ]
    for load in loads:
        load.start()

    tokens = tokens_ref[...]
    values = tokens.astype(jnp.float32)
    ones = group_ones(channels)
    total = jnp.sum(values, axis=0, keepdims=True)
    squares = jnp.sum(values * values, axis=0, keepdims=True)
    summed = jnp.concatenate([total, squares, jnp.zeros((6, channels), jnp.float32)], axis=0)
    total_ref[...] = sum(dot(piece, ones) for piece in pieces(summed, 3))
    pl.semaphore_wait(barrier, count - 1 + chips)
    stats_pairs = [(total_ref, totals_ref)]
    to_later(count, stats_pairs, total_send, total_recv)

    rate, angle = rate_ref[...], angle_ref[...]
    size = jnp.exp(-rate)
    turn_re = size * jnp.cos(angle)
    turn_im = size * jnp.sin(angle)
    weight = (1.0 - size) * input_ref[...]
    read_re = weight * output_ref[0]
    read_im = weight * output_ref[1]
    power_re, power_im = jnp.ones_like(rate), jnp.zeros_like(rate)
    lag_rows = []
    for lag in range(STEPS + 1):
        if lag < STEPS:
            lag_rows.append(jnp.sum(read_re * power_re - read_im * power_im, axis=0, keepdims=True))
        power_ref[0, lag] = power_re
        power_ref[1, lag] = power_im
        power_re, power_im = power_re * turn_re - power_im * turn_im, power_re * turn_im + power_im * turn_re
    unit_ref[0] = read_re * turn_re - read_im * turn_im
    unit_ref[1] = read_re * turn_im + read_im * turn_re
    step_row = lax.broadcasted_iota(jnp.int32, (STEPS, channels), 0)

    def table(part, carried):
        here = pl.ds(part, 1)
        re = jnp.broadcast_to(unit_ref[0, here, :], (STEPS, channels))
        im = jnp.broadcast_to(unit_ref[1, here, :], (STEPS, channels))
        for bit in (1, 2, 4):
            chosen = (step_row // bit) % 2 == 1
            by_re = jnp.where(chosen, jnp.broadcast_to(power_ref[0, bit, here, :], (STEPS, channels)), 1.0)
            by_im = jnp.where(chosen, jnp.broadcast_to(power_ref[1, bit, here, :], (STEPS, channels)), 0.0)
            re, im = re * by_re - im * by_im, re * by_im + im * by_re
        read_ref[0, part] = re
        read_ref[1, part] = im
        return carried

    lax.fori_loop(0, ndim, table, 0)

    sums = dot(tokens, ones)
    squares = sum(dot(piece, ones) for piece in pieces(values * values, 2))
    row = lax.broadcasted_iota(jnp.int32, (length, length), 0)
    column = lax.broadcasted_iota(jnp.int32, (length, length), 1)
    lower = (column <= row).astype(jnp.bfloat16)
    cum_sum = sum(dot(lower, piece) for piece in pieces(sums, 3))
    cum_sq = sum(dot(lower, piece) for piece in pieces(squares, 3))
    diagonal = jnp.where(row == column, jnp.broadcast_to(retain_ref[...], (length, length)), 0.0)
    keep = sum(dot(piece, jnp.ones((length, LANES), jnp.bfloat16)) for piece in pieces(diagonal, 3))
    place_in = lax.broadcasted_iota(jnp.int32, (length, LANES), 0) % STEPS
    prefix = keep
    suffix = jnp.where(place_in < STEPS - 1, pltpu.roll(keep, length - 1, 0), 1.0)
    for by in (1, 2, 4):
        prefix = jnp.where(place_in >= by, prefix * pltpu.roll(prefix, by, 0), prefix)
        suffix = jnp.where(place_in + by < STEPS, suffix * pltpu.roll(suffix, length - by, 0), suffix)
    prefix_ref[...] = prefix
    position = lax.broadcasted_iota(jnp.int32, (length, channels), 0)
    counts = ((span * length + position + 1) * GROUP).astype(jnp.float32)

    from_earlier(count, stats_pairs, total_send, total_recv)
    before_ref[...] = jnp.zeros((8, channels), jnp.float32)
    for other in range(count - 1):

        @pl.when(other < span)
        def _():
            before_ref[...] += totals_ref[other]

    average = (before_ref[0:1] + cum_sum) / counts
    spread = (before_ref[1:2] + cum_sq) / counts - average * average
    inverse = lax.rsqrt(spread + NORM_EPS)
    normed = (values - average) * inverse * norm_gain_ref[...] + bias_ref[...]
    normed_ref[...] = normed
    scaled_ref[...] = normed * wide(suffix, channels)

    width = min(256, channels)
    for lanes in lanes_of(channels, width):
        whole_re, whole_im = power_ref[0, STEPS, :, lanes], power_ref[1, STEPS, :, lanes]

        def enter(block, carried):
            re, im, kept = carried
            start_ref[0, block, :, lanes] = re
            start_ref[1, block, :, lanes] = im
            first = pl.multiple_of(block * STEPS, STEPS)
            factor = wide(prefix_ref[pl.ds(first + STEPS - 1, 1), :], width)
            add_re = jnp.broadcast_to(scaled_ref[pl.ds(first + STEPS - 1, 1), lanes], (ndim, width))
            add_im = jnp.zeros((ndim, width), jnp.float32)
            for step in range(STEPS - 1):
                entry = scaled_ref[pl.ds(first + step, 1), lanes]
                lag = STEPS - 1 - step
                add_re = add_re + power_ref[0, lag, :, lanes] * entry
                add_im = add_im + power_ref[1, lag, :, lanes] * entry
            next_re = (whole_re * re - whole_im * im) * factor + add_re
            next_im = (whole_re * im + whole_im * re) * factor + add_im
            return next_re, next_im, kept * factor

        zero = jnp.zeros((ndim, width), jnp.float32)
        re, im, kept = lax.fori_loop(0, blocks, enter, (zero, zero, jnp.ones((1, width), jnp.float32)))
        state_ref[0:ndim, lanes] = re.astype(state_ref.dtype)
        state_ref[ndim : 2 * ndim, lanes] = im.astype(state_ref.dtype)
    kept_ref[...] = jnp.broadcast_to(kept[:, :LANES], (8, LANES))
    state_pairs = [(state_ref, states_ref), (kept_ref, kepts_ref)]
    to_later(count, state_pairs, state_send, state_recv)

    for lanes in lanes_of(channels, LANES):
        reach = jnp.where(place_in >= 0, 1.0, 0.0)
        here = normed_ref[:, lanes]
        within = here * lag_rows[0][:, lanes]
        for lag in range(1, STEPS):
            reach = jnp.where(place_in >= lag, reach * (pltpu.roll(keep, lag - 1, 0) if lag > 1 else keep), 0.0)
            within = within + pltpu.roll(here, lag, 0) * (lag_rows[lag][:, lanes] * reach)
        ema_ref[:, lanes] = within + skip_ref[:, lanes] * here

    from_earlier(count, state_pairs, state_send, state_recv)
    whole = jnp.exp(-rate * length)
    unit_ref[0] = whole * jnp.cos(angle * length)
    unit_ref[1] = whole * jnp.sin(angle * length)
    power_ref[0, 0] = jnp.zeros_like(rate)
    power_ref[1, 0] = jnp.zeros_like(rate)
    for other in range(count - 1):

        @pl.when(other < span)
        def _():
            kept = wide(kepts_ref[other, 0:1, :], channels)
            re, im = power_ref[0, 0], power_ref[1, 0]
            by_re, by_im = unit_ref[0], unit_ref[1]
            power_ref[0, 0] = (by_re * re - by_im * im) * kept + states_ref[other, 0:ndim].astype(jnp.float32)
            power_ref[1, 0] = (by_re * im + by_im * re) * kept + states_ref[other, ndim : 2 * ndim].astype(jnp.float32)

    for lanes in lanes_of(channels, width):
        whole_re, whole_im = power_ref[0, STEPS, :, lanes], power_ref[1, STEPS, :, lanes]

        def leave(block, carried):
            re, im = carried
            first = pl.multiple_of(block * STEPS, STEPS)
            parts = [jnp.zeros((STEPS, width), jnp.float32) for _ in range(4)]
            for part in range(ndim):
                here = pl.ds(part, 1)
                slot = 2 * (part % 2)
                parts[slot] = parts[slot] + read_ref[0, part, :, lanes] * start_ref[0, block, here, lanes]
                parts[slot + 1] = parts[slot + 1] + read_ref[1, part, :, lanes] * start_ref[1, block, here, lanes]
            read = (parts[0] - parts[1]) + (parts[2] - parts[3])
            ema_ref[pl.ds(first, STEPS), lanes] += read * wide(prefix_ref[pl.ds(first, STEPS), :], width)
            factor = wide(prefix_ref[pl.ds(first + STEPS - 1, 1), :], width)
            re, im = (whole_re * re - whole_im * im) * factor, (whole_re * im + whole_im * re) * factor
            start_ref[0, block + 1, :, lanes] += re
            start_ref[1, block + 1, :, lanes] += im
            return re, im

        re, im = power_ref[0, 0, :, lanes], power_ref[1, 0, :, lanes]
        start_ref[0, 0, :, lanes] += re
        start_ref[1, 0, :, lanes] += im
        start_ref[0, blocks, :, lanes] = re
        start_ref[1, blocks, :, lanes] = im
        lax.fori_loop(0, blocks, leave, (re, im))

    ema = ema_ref[...]
    active = (ema / (1.0 + jnp.exp(-ema))).astype(jnp.bfloat16)
    for load in loads:
        load.wait()
    product = dot(active, weight_ref[...]).astype(jnp.bfloat16)
    part_ref[...] = product.reshape(part_ref.shape)

    pair, far, outward, home, back = {}, {}, {}, {}, {}
    for half in range(halves):
        for slot, place in enumerate(order):
            copy = remote(part_ref.at[place, 1 - core, half], near_ref.at[slot, half], pair_send.at[slot, half], pair_recv.at[slot, half], "tensor", partner)
            copy.start()
            pair[slot, half] = copy
    for half in range(halves):
        for slot, place in enumerate(order[:-1]):
            pair[slot, half].wait_recv()
            added = part_ref[place, core, half].astype(jnp.float32) + near_ref[slot, half].astype(jnp.float32)
            sum_ref[slot, half] = added.astype(jnp.bfloat16)
            copy = remote(sum_ref.at[slot, half], far_ref.at[slot, half], far_send.at[slot, half], far_recv.at[slot, half], "tensor", peers[slot])
            copy.start()
            far[slot, half] = copy
    for half in range(halves):
        pair[chips - 1, half].wait_recv()
        shared = part_ref[chip, core, half].astype(jnp.float32) + near_ref[chips - 1, half].astype(jnp.float32)
        for slot in range(chips - 1):
            far[slot, half].wait_recv()
            shared = shared + far_ref[slot, half].astype(jnp.float32)
        squares = jnp.mean(shared * shared, axis=1, keepdims=True)
        own_ref[half] = (shared * lax.rsqrt(squares + SCALE_EPS) * gain_ref[...]).astype(jnp.bfloat16)
        landing = all_ref.at[chip, core, half]
        for slot in range(chips - 1):
            copy = remote(own_ref.at[half], landing, out_send.at[slot, half], out_recv.at[slot, half], "tensor", peers[slot])
            copy.start()
            outward[slot, half] = copy
        copy = remote(own_ref.at[half], landing, back_send.at[chips - 1, half], back_recv.at[chips - 1, half], "tensor", partner)
        copy.start()
        home[half] = copy
        all_ref[chip, core, half] = own_ref[half]
    columns = all_ref.shape[4]

    def finish(place):
        gathered = all_ref[place].reshape(2 * halves * rows, columns)
        out_ref[place] = dot(gathered, mixer_ref[...]).astype(jnp.bfloat16)

    def origin(slot):
        return lax.rem(chip + chips - 1 - slot, chips)

    def close(slot):
        for half in range(halves):
            back[slot, half].wait_recv()
        finish(origin(slot))

    for half in range(halves):
        home[half].wait_recv()
    finish(chip)
    for half in range(halves):
        for slot in range(chips - 1):
            outward[slot, half].wait_recv()
            block = all_ref.at[origin(slot), core, half]
            copy = remote(block, block, back_send.at[slot, half], back_recv.at[slot, half], "tensor", partner)
            copy.start()
            back[slot, half] = copy
            if slot and half == halves - 1:
                close(slot - 1)
    close(chips - 2)
    for copies in (pair, far, outward, home, back):
        for copy in copies.values():
            copy.wait_send()


def layer(tokens, retain, norm_gain, norm_bias, rate, angle, source, output, skip, weight, gain, mixer):
    length, channels = tokens.shape
    ndim = rate.shape[0]
    blocks = length // STEPS
    count = lax.axis_size("span")
    chips = lax.axis_size("tensor") // 2
    rows, columns = length // (2 * chips), weight.shape[1]
    halves = 2 if rows % 32 == 0 else 1
    block = (halves, rows // halves, columns)
    f32, bf16 = jnp.float32, jnp.bfloat16
    sems = pltpu.SemaphoreType.DMA
    hbm = pl.BlockSpec(memory_space=pltpu.HBM)
    out = pl.pallas_call(
        functools.partial(layer_kernel, count, chips),
        out_shape=jax.ShapeDtypeStruct((chips, 2 * rows, mixer.shape[1]), bf16),
        in_specs=[VMEM] * 10 + [hbm, hbm],
        out_specs=VMEM,
        scratch_shapes=[
            pltpu.VMEM(weight.shape, bf16),
            pltpu.VMEM(mixer.shape, bf16),
            pltpu.VMEM((8, channels), f32),
            pltpu.VMEM((count, 8, channels), f32),
            pltpu.VMEM((8, channels), f32),
            pltpu.VMEM((length, channels), f32),
            pltpu.VMEM((length, channels), f32),
            pltpu.VMEM((length, LANES), f32),
            pltpu.VMEM((2, STEPS + 1, ndim, channels), f32),
            pltpu.VMEM((2, ndim, channels), f32),
            pltpu.VMEM((2, ndim, STEPS, channels), f32),
            pltpu.VMEM((2, blocks + 1, ndim, channels), f32),
            pltpu.VMEM((2 * ndim, channels), bf16),
            pltpu.VMEM((count, 2 * ndim, channels), bf16),
            pltpu.VMEM((8, LANES), f32),
            pltpu.VMEM((count, 8, LANES), f32),
            pltpu.VMEM((length, channels), f32),
            pltpu.VMEM((chips, 2) + block, bf16),
            pltpu.VMEM((chips,) + block, bf16),
            pltpu.VMEM((chips - 1,) + block, bf16),
            pltpu.VMEM((chips - 1,) + block, bf16),
            pltpu.VMEM(block, bf16),
            pltpu.VMEM((chips, 2) + block, bf16),
            sems((2,)),
            sems((1, count - 1)),
            sems((1, count - 1)),
            sems((2, count - 1)),
            sems((2, count - 1)),
            sems((chips, halves)),
            sems((chips, halves)),
            sems((chips - 1, halves)),
            sems((chips - 1, halves)),
            sems((chips - 1, halves)),
            sems((chips - 1, halves)),
            sems((chips, halves)),
            sems((chips, halves)),
        ],
        compiler_params=pltpu.CompilerParams(collective_id=0, has_side_effects=True),
        name="layer",
    )(
        tokens,
        retain.reshape(1, -1),
        norm_gain.reshape(1, -1),
        norm_bias.reshape(1, -1),
        rate,
        angle,
        source,
        output,
        skip.reshape(1, -1),
        gain.reshape(1, -1),
        weight,
        mixer,
    )
    return out.reshape(length, mixer.shape[1])


def solution(mesh):
    in_specs = (
        P("span", "tensor"),
        P("span"),
        P("tensor"),
        P("tensor"),
        P(None, "tensor"),
        P(None, "tensor"),
        P(None, "tensor"),
        P(None, None, "tensor"),
        P("tensor"),
        P("tensor", None),
        P(),
        P(None, "tensor"),
    )
    return jax.shard_map(layer, mesh=mesh, in_specs=in_specs, out_specs=P("span", "tensor"), check_vma=False)
```

```python
import functools

import jax
import jax.numpy as jnp
from jax import lax
from jax.experimental import pallas as pl
from jax.experimental.pallas import tpu as pltpu
from jax.sharding import PartitionSpec as P

GROUP = 64
STEPS = 8
LANES = 128
NORM_EPS = 1e-05
SCALE_EPS = 1e-06

MESH = pl.DeviceIdType.MESH
VMEM = pl.BlockSpec(memory_space=pltpu.VMEM)


def dot(a, b):
    return jnp.dot(a, b, preferred_element_type=jnp.float32)


def pieces(values, count):
    out = []
    for _ in range(count):
        piece = values.astype(jnp.bfloat16)
        out.append(piece)
        values = values - piece.astype(jnp.float32)
    return out


def group_ones(channels):
    row = lax.broadcasted_iota(jnp.int32, (channels, channels), 0) // GROUP
    column = lax.broadcasted_iota(jnp.int32, (channels, channels), 1) // GROUP
    return (row == column).astype(jnp.bfloat16)


def remote(source, target, send_sem, recv_sem, axis, device):
    return pltpu.make_async_remote_copy(
        src_ref=source,
        dst_ref=target,
        send_sem=send_sem,
        recv_sem=recv_sem,
        device_id={axis: device},
        device_id_type=MESH,
    )


def to_later(count, pairs, send_sem, recv_sem):
    me = lax.axis_index("span")
    for step in range(1, count):

        @pl.when(me + step < count)
        def _():
            for item, (source, landing) in enumerate(pairs):
                remote(source, landing.at[me], send_sem.at[item, step - 1], recv_sem.at[item, step - 1], "span", me + step).start()


def from_earlier(count, pairs, send_sem, recv_sem):
    me = lax.axis_index("span")
    for step in range(1, count):

        @pl.when(me >= step)
        def _():
            for item, (source, landing) in enumerate(pairs):
                remote(source, landing.at[me], send_sem.at[item, step - 1], recv_sem.at[item, step - 1], "span", me - step).wait_recv()

        @pl.when(me + step < count)
        def _():
            for item, (source, landing) in enumerate(pairs):
                remote(source, landing.at[me], send_sem.at[item, step - 1], recv_sem.at[item, step - 1], "span", me + step).wait_send()


def wide(column, width):
    return jnp.concatenate([column] * (width // LANES), axis=1)


def lanes_of(channels, width):
    return [slice(start, start + width) for start in range(0, channels, width)]


def layer_kernel(
    count,
    chips,
    tokens_ref,
    retain_ref,
    norm_gain_ref,
    bias_ref,
    rate_ref,
    angle_ref,
    input_ref,
    output_ref,
    skip_ref,
    gain_ref,
    weight_hbm,
    mixer_hbm,
    out_ref,
    weight_ref,
    mixer_ref,
    total_ref,
    totals_ref,
    before_ref,
    normed_ref,
    scaled_ref,
    prefix_ref,
    power_ref,
    unit_ref,
    read_ref,
    start_ref,
    state_ref,
    states_ref,
    kept_ref,
    kepts_ref,
    ema_ref,
    part_ref,
    near_ref,
    sum_ref,
    far_ref,
    own_ref,
    all_ref,
    load_sem,
    total_send,
    total_recv,
    state_send,
    state_recv,
    pair_send,
    pair_recv,
    far_send,
    far_recv,
    out_send,
    out_recv,
    back_send,
    back_recv,
):
    length, channels = tokens_ref.shape
    ndim = rate_ref.shape[0]
    blocks = length // STEPS
    halves, rows = part_ref.shape[2:4]
    span = lax.axis_index("span")
    me = lax.axis_index("tensor")
    core = lax.rem(me, 2)
    chip = lax.div(me, 2)
    partner = me + 1 - 2 * core
    order = [lax.rem(chip + step, chips) for step in range(1, chips)] + [chip]
    peers = [2 * place + core for place in order[:-1]]

    barrier = pltpu.get_barrier_semaphore()
    for step in range(1, count):
        pl.semaphore_signal(barrier, inc=1, device_id={"span": lax.rem(span + step, count)}, device_id_type=MESH)
    for peer in [partner] + peers:
        pl.semaphore_signal(barrier, inc=1, device_id={"tensor": peer}, device_id_type=MESH)
    loads = [
        pltpu.make_async_copy(weight_hbm, weight_ref, load_sem.at[0]),
        pltpu.make_async_copy(mixer_hbm, mixer_ref, load_sem.at[1]),
    ]
    for load in loads:
        load.start()

    tokens = tokens_ref[...]
    values = tokens.astype(jnp.float32)
    ones = group_ones(channels)
    total = jnp.sum(values, axis=0, keepdims=True)
    squares = jnp.sum(values * values, axis=0, keepdims=True)
    summed = jnp.concatenate([total, squares, jnp.zeros((6, channels), jnp.float32)], axis=0)
    total_ref[...] = sum(dot(piece, ones) for piece in pieces(summed, 3))
    pl.semaphore_wait(barrier, count - 1 + chips)
    stats_pairs = [(total_ref, totals_ref)]
    to_later(count, stats_pairs, total_send, total_recv)

    rate, angle = rate_ref[...], angle_ref[...]
    size = jnp.exp(-rate)
    turn_re = size * jnp.cos(angle)
    turn_im = size * jnp.sin(angle)
    weight = (1.0 - size) * input_ref[...]
    read_re = weight * output_ref[0]
    read_im = weight * output_ref[1]
    power_re, power_im = jnp.ones_like(rate), jnp.zeros_like(rate)
    lag_rows = []
    for lag in range(STEPS + 1):
        if lag < STEPS:
            lag_rows.append(jnp.sum(read_re * power_re - read_im * power_im, axis=0, keepdims=True))
        power_ref[0, lag] = power_re
        power_ref[1, lag] = power_im
        power_re, power_im = power_re * turn_re - power_im * turn_im, power_re * turn_im + power_im * turn_re
    unit_ref[0] = read_re * turn_re - read_im * turn_im
    unit_ref[1] = read_re * turn_im + read_im * turn_re
    step_row = lax.broadcasted_iota(jnp.int32, (STEPS, channels), 0)

    def table(part, carried):
        here = pl.ds(part, 1)
        re = jnp.broadcast_to(unit_ref[0, here, :], (STEPS, channels))
        im = jnp.broadcast_to(unit_ref[1, here, :], (STEPS, channels))
        for bit in (1, 2, 4):
            chosen = (step_row // bit) % 2 == 1
            by_re = jnp.where(chosen, jnp.broadcast_to(power_ref[0, bit, here, :], (STEPS, channels)), 1.0)
            by_im = jnp.where(chosen, jnp.broadcast_to(power_ref[1, bit, here, :], (STEPS, channels)), 0.0)
            re, im = re * by_re - im * by_im, re * by_im + im * by_re
        read_ref[0, part] = re
        read_ref[1, part] = im
        return carried

    lax.fori_loop(0, ndim, table, 0)

    sums = dot(tokens, ones)
    squares = sum(dot(piece, ones) for piece in pieces(values * values, 2))
    row = lax.broadcasted_iota(jnp.int32, (length, length), 0)
    column = lax.broadcasted_iota(jnp.int32, (length, length), 1)
    lower = (column <= row).astype(jnp.bfloat16)
    cum_sum = sum(dot(lower, piece) for piece in pieces(sums, 3))
    cum_sq = sum(dot(lower, piece) for piece in pieces(squares, 3))
    diagonal = jnp.where(row == column, jnp.broadcast_to(retain_ref[...], (length, length)), 0.0)
    keep = sum(dot(piece, jnp.ones((length, LANES), jnp.bfloat16)) for piece in pieces(diagonal, 3))
    place_in = lax.broadcasted_iota(jnp.int32, (length, LANES), 0) % STEPS
    prefix = keep
    suffix = jnp.where(place_in < STEPS - 1, pltpu.roll(keep, length - 1, 0), 1.0)
    for by in (1, 2, 4):
        prefix = jnp.where(place_in >= by, prefix * pltpu.roll(prefix, by, 0), prefix)
        suffix = jnp.where(place_in + by < STEPS, suffix * pltpu.roll(suffix, length - by, 0), suffix)
    prefix_ref[...] = prefix
    position = lax.broadcasted_iota(jnp.int32, (length, channels), 0)
    counts = ((span * length + position + 1) * GROUP).astype(jnp.float32)

    from_earlier(count, stats_pairs, total_send, total_recv)
    before_ref[...] = jnp.zeros((8, channels), jnp.float32)
    for other in range(count - 1):

        @pl.when(other < span)
        def _():
            before_ref[...] += totals_ref[other]

    average = (before_ref[0:1] + cum_sum) / counts
    spread = (before_ref[1:2] + cum_sq) / counts - average * average
    inverse = lax.rsqrt(spread + NORM_EPS)
    normed = (values - average) * inverse * norm_gain_ref[...] + bias_ref[...]
    normed_ref[...] = normed
    scaled_ref[...] = normed * wide(suffix, channels)

    width = min(512, channels)
    for lanes in lanes_of(channels, width):
        whole_re, whole_im = power_ref[0, STEPS, :, lanes], power_ref[1, STEPS, :, lanes]

        def enter(block, carried):
            re, im, kept = carried
            start_ref[0, block, :, lanes] = re
            start_ref[1, block, :, lanes] = im
            first = pl.multiple_of(block * STEPS, STEPS)
            factor = wide(prefix_ref[pl.ds(first + STEPS - 1, 1), :], width)
            add_re = jnp.broadcast_to(scaled_ref[pl.ds(first + STEPS - 1, 1), lanes], (ndim, width))
            add_im = jnp.zeros((ndim, width), jnp.float32)
            for step in range(STEPS - 1):
                entry = scaled_ref[pl.ds(first + step, 1), lanes]
                lag = STEPS - 1 - step
                add_re = add_re + power_ref[0, lag, :, lanes] * entry
                add_im = add_im + power_ref[1, lag, :, lanes] * entry
            next_re = (whole_re * re - whole_im * im) * factor + add_re
            next_im = (whole_re * im + whole_im * re) * factor + add_im
            return next_re, next_im, kept * factor

        zero = jnp.zeros((ndim, width), jnp.float32)
        re, im, kept = lax.fori_loop(0, blocks, enter, (zero, zero, jnp.ones((1, width), jnp.float32)))
        state_ref[0:ndim, lanes] = re.astype(state_ref.dtype)
        state_ref[ndim : 2 * ndim, lanes] = im.astype(state_ref.dtype)
    kept_ref[...] = jnp.broadcast_to(kept[:, :LANES], (8, LANES))
    state_pairs = [(state_ref, states_ref), (kept_ref, kepts_ref)]
    to_later(count, state_pairs, state_send, state_recv)

    for lanes in lanes_of(channels, LANES):
        reach = jnp.where(place_in >= 0, 1.0, 0.0)
        here = normed_ref[:, lanes]
        within = here * lag_rows[0][:, lanes]
        for lag in range(1, STEPS):
            reach = jnp.where(place_in >= lag, reach * (pltpu.roll(keep, lag - 1, 0) if lag > 1 else keep), 0.0)
            within = within + pltpu.roll(here, lag, 0) * (lag_rows[lag][:, lanes] * reach)
        ema_ref[:, lanes] = within + skip_ref[:, lanes] * here

    from_earlier(count, state_pairs, state_send, state_recv)
    whole = jnp.exp(-rate * length)
    unit_ref[0] = whole * jnp.cos(angle * length)
    unit_ref[1] = whole * jnp.sin(angle * length)
    power_ref[0, 0] = jnp.zeros_like(rate)
    power_ref[1, 0] = jnp.zeros_like(rate)
    for other in range(count - 1):

        @pl.when(other < span)
        def _():
            kept = wide(kepts_ref[other, 0:1, :], channels)
            re, im = power_ref[0, 0], power_ref[1, 0]
            by_re, by_im = unit_ref[0], unit_ref[1]
            power_ref[0, 0] = (by_re * re - by_im * im) * kept + states_ref[other, 0:ndim].astype(jnp.float32)
            power_ref[1, 0] = (by_re * im + by_im * re) * kept + states_ref[other, ndim : 2 * ndim].astype(jnp.float32)

    width = min(256, channels)
    for lanes in lanes_of(channels, width):
        whole_re, whole_im = power_ref[0, STEPS, :, lanes], power_ref[1, STEPS, :, lanes]

        def leave(block, carried):
            re, im = carried
            first = pl.multiple_of(block * STEPS, STEPS)
            parts = [jnp.zeros((STEPS, width), jnp.float32) for _ in range(4)]
            for part in range(ndim):
                here = pl.ds(part, 1)
                slot = 2 * (part % 2)
                parts[slot] = parts[slot] + read_ref[0, part, :, lanes] * start_ref[0, block, here, lanes]
                parts[slot + 1] = parts[slot + 1] + read_ref[1, part, :, lanes] * start_ref[1, block, here, lanes]
            read = (parts[0] - parts[1]) + (parts[2] - parts[3])
            ema_ref[pl.ds(first, STEPS), lanes] += read * wide(prefix_ref[pl.ds(first, STEPS), :], width)
            factor = wide(prefix_ref[pl.ds(first + STEPS - 1, 1), :], width)
            re, im = (whole_re * re - whole_im * im) * factor, (whole_re * im + whole_im * re) * factor
            start_ref[0, block + 1, :, lanes] += re
            start_ref[1, block + 1, :, lanes] += im
            return re, im

        re, im = power_ref[0, 0, :, lanes], power_ref[1, 0, :, lanes]
        start_ref[0, 0, :, lanes] += re
        start_ref[1, 0, :, lanes] += im
        start_ref[0, blocks, :, lanes] = re
        start_ref[1, blocks, :, lanes] = im
        lax.fori_loop(0, blocks, leave, (re, im), unroll=2)

    ema = ema_ref[...]
    active = (ema / (1.0 + jnp.exp(-ema))).astype(jnp.bfloat16)
    for load in loads:
        load.wait()
    product = dot(active, weight_ref[...]).astype(jnp.bfloat16)
    part_ref[...] = product.reshape(part_ref.shape)

    pair, far, outward, home, back = {}, {}, {}, {}, {}
    for half in range(halves):
        for slot, place in enumerate(order):
            copy = remote(part_ref.at[place, 1 - core, half], near_ref.at[slot, half], pair_send.at[slot, half], pair_recv.at[slot, half], "tensor", partner)
            copy.start()
            pair[slot, half] = copy
    for half in range(halves):
        for slot, place in enumerate(order[:-1]):
            pair[slot, half].wait_recv()
            added = part_ref[place, core, half].astype(jnp.float32) + near_ref[slot, half].astype(jnp.float32)
            sum_ref[slot, half] = added.astype(jnp.bfloat16)
            copy = remote(sum_ref.at[slot, half], far_ref.at[slot, half], far_send.at[slot, half], far_recv.at[slot, half], "tensor", peers[slot])
            copy.start()
            far[slot, half] = copy
    for half in range(halves):
        pair[chips - 1, half].wait_recv()
        shared = part_ref[chip, core, half].astype(jnp.float32) + near_ref[chips - 1, half].astype(jnp.float32)
        for slot in range(chips - 1):
            far[slot, half].wait_recv()
            shared = shared + far_ref[slot, half].astype(jnp.float32)
        squares = jnp.mean(shared * shared, axis=1, keepdims=True)
        own_ref[half] = (shared * lax.rsqrt(squares + SCALE_EPS) * gain_ref[...]).astype(jnp.bfloat16)
        landing = all_ref.at[chip, core, half]
        for slot in range(chips - 1):
            copy = remote(own_ref.at[half], landing, out_send.at[slot, half], out_recv.at[slot, half], "tensor", peers[slot])
            copy.start()
            outward[slot, half] = copy
        copy = remote(own_ref.at[half], landing, back_send.at[chips - 1, half], back_recv.at[chips - 1, half], "tensor", partner)
        copy.start()
        home[half] = copy
        all_ref[chip, core, half] = own_ref[half]
    columns = all_ref.shape[4]

    def finish(place):
        gathered = all_ref[place].reshape(2 * halves * rows, columns)
        out_ref[place] = dot(gathered, mixer_ref[...]).astype(jnp.bfloat16)

    def origin(slot):
        return lax.rem(chip + chips - 1 - slot, chips)

    def close(slot):
        for half in range(halves):
            back[slot, half].wait_recv()
        finish(origin(slot))

    for half in range(halves):
        home[half].wait_recv()
    finish(chip)
    for half in range(halves):
        for slot in range(chips - 1):
            outward[slot, half].wait_recv()
            block = all_ref.at[origin(slot), core, half]
            copy = remote(block, block, back_send.at[slot, half], back_recv.at[slot, half], "tensor", partner)
            copy.start()
            back[slot, half] = copy
            if slot and half == halves - 1:
                close(slot - 1)
    close(chips - 2)
    for copies in (pair, far, outward, home, back):
        for copy in copies.values():
            copy.wait_send()


def layer(tokens, retain, norm_gain, norm_bias, rate, angle, source, output, skip, weight, gain, mixer):
    length, channels = tokens.shape
    ndim = rate.shape[0]
    blocks = length // STEPS
    count = lax.axis_size("span")
    chips = lax.axis_size("tensor") // 2
    rows, columns = length // (2 * chips), weight.shape[1]
    halves = 2 if rows % 32 == 0 else 1
    block = (halves, rows // halves, columns)
    f32, bf16 = jnp.float32, jnp.bfloat16
    sems = pltpu.SemaphoreType.DMA
    hbm = pl.BlockSpec(memory_space=pltpu.HBM)
    out = pl.pallas_call(
        functools.partial(layer_kernel, count, chips),
        out_shape=jax.ShapeDtypeStruct((chips, 2 * rows, mixer.shape[1]), bf16),
        in_specs=[VMEM] * 10 + [hbm, hbm],
        out_specs=VMEM,
        scratch_shapes=[
            pltpu.VMEM(weight.shape, bf16),
            pltpu.VMEM(mixer.shape, bf16),
            pltpu.VMEM((8, channels), f32),
            pltpu.VMEM((count, 8, channels), f32),
            pltpu.VMEM((8, channels), f32),
            pltpu.VMEM((length, channels), f32),
            pltpu.VMEM((length, channels), f32),
            pltpu.VMEM((length, LANES), f32),
            pltpu.VMEM((2, STEPS + 1, ndim, channels), f32),
            pltpu.VMEM((2, ndim, channels), f32),
            pltpu.VMEM((2, ndim, STEPS, channels), f32),
            pltpu.VMEM((2, blocks + 1, ndim, channels), f32),
            pltpu.VMEM((2 * ndim, channels), bf16),
            pltpu.VMEM((count, 2 * ndim, channels), bf16),
            pltpu.VMEM((8, LANES), f32),
            pltpu.VMEM((count, 8, LANES), f32),
            pltpu.VMEM((length, channels), f32),
            pltpu.VMEM((chips, 2) + block, bf16),
            pltpu.VMEM((chips,) + block, bf16),
            pltpu.VMEM((chips - 1,) + block, bf16),
            pltpu.VMEM((chips - 1,) + block, bf16),
            pltpu.VMEM(block, bf16),
            pltpu.VMEM((chips, 2) + block, bf16),
            sems((2,)),
            sems((1, count - 1)),
            sems((1, count - 1)),
            sems((2, count - 1)),
            sems((2, count - 1)),
            sems((chips, halves)),
            sems((chips, halves)),
            sems((chips - 1, halves)),
            sems((chips - 1, halves)),
            sems((chips - 1, halves)),
            sems((chips - 1, halves)),
            sems((chips, halves)),
            sems((chips, halves)),
        ],
        compiler_params=pltpu.CompilerParams(collective_id=0, has_side_effects=True),
        name="layer",
    )(
        tokens,
        retain.reshape(1, -1),
        norm_gain.reshape(1, -1),
        norm_bias.reshape(1, -1),
        rate,
        angle,
        source,
        output,
        skip.reshape(1, -1),
        gain.reshape(1, -1),
        weight,
        mixer,
    )
    return out.reshape(length, mixer.shape[1])


def solution(mesh):
    in_specs = (
        P("span", "tensor"),
        P("span"),
        P("tensor"),
        P("tensor"),
        P(None, "tensor"),
        P(None, "tensor"),
        P(None, "tensor"),
        P(None, None, "tensor"),
        P("tensor"),
        P("tensor", None),
        P(),
        P(None, "tensor"),
    )
    return jax.shard_map(layer, mesh=mesh, in_specs=in_specs, out_specs=P("span", "tensor"), check_vma=False)
```
